128 devices in a mesh: fsdp: 8 (over z_lo, x), dp: 4 (over y), cand: 4 (over z_hi, core).
Axes of the slice: x: 4, y: 4, z: 4 (z_hi: 2, z_lo: 2; z = z_hi * 2 + z_lo), core: 2. Of those that a mesh axis runs over, the one named last changes fastest.
Arguments:
- tokens: bfloat16 [640, 8192], P(('dp', 'cand'), 'fsdp'), may hold values from -6 to 6
- cotangent: bfloat16 [640, 8192], P(('dp', 'cand'), 'fsdp'), may hold values from -6 to 6
- bleu_gains: int32 [4, 8], P('dp', 'cand'), may hold values from 0 to 9600, as said below
- gate_weight: bfloat16 [8192, 29568], P('fsdp', ('dp', 'cand')), may hold values from -0.0625 to 0.0625
- up_weight: bfloat16 [8192, 29568], P('fsdp', ('dp', 'cand')), may hold values from -0.0625 to 0.0625
- down_weight: bfloat16 [29568, 8192], P(('dp', 'cand'), 'fsdp'), may hold values from -0.03125 to 0.03125
Outputs:
- layer_out: bfloat16 [640, 8192], P(('dp', 'cand'), 'fsdp')
- grad_tokens: bfloat16 [640, 8192], P(('dp', 'cand'), 'fsdp')
- grad_gate_weight: bfloat16 [8192, 29568], P('fsdp', ('dp', 'cand'))
- grad_up_weight: bfloat16 [8192, 29568], P('fsdp', ('dp', 'cand'))
- grad_down_weight: bfloat16 [29568, 8192], P(('dp', 'cand'), 'fsdp')
The draws below stay inside these ranges and needn't reach their ends.
Inputs may be any that keep to these rules, and one draw needn't show every extreme that they name: `bleu_gains`: BLEU gain of a candidate in parts per ten thousand.
All inputs are finite; a program needn't handle non-finite values.
Results may differ from the reference program's by a relative error of at most 0.0058.
Values may be sent and summed in bfloat16 or wider, within the bound.
No kernel may reach another device: no remote copies, remote signals or barrier semaphores. Data moves between devices by JAX's collectives and lax.ppermute only.
A program may use at most 128 MiB of HBM per device.

```python
import jax
import jax.numpy as jnp

D = 8192
FF = 29568
CANDS = 8
LEN = 20
SOURCES = 4
TOKENS = 640


def draw_bleu_gains(key, part):
    base_gain = jax.random.randint(key, (SOURCES, CANDS), 0, 1201)
    ladder = 1200 * jnp.arange(CANDS, dtype=jnp.int32)
    return (base_gain + ladder[None, :]).astype(jnp.int32)


def level_of(stream_key, dims, split, least, top_value):
    level = 1.0
    for dim, blocks in split:
        steps = jax.random.uniform(jax.random.fold_in(jax.random.fold_in(stream_key, 6), dim), (blocks,), jnp.float32, least / len(split), top_value / len(split))
        level = level * jnp.repeat(jnp.exp(steps), dims[dim] // blocks).reshape((-1,) + (1,) * (len(dims) - 1 - dim))
    return level


def normal_values(rng, dims, scale, bound, pieces=(), held_as=jnp.bfloat16):
    factor_of = level_of(rng, dims, pieces, -0.22, 0.18) if pieces else 1.0
    result = jax.random.normal(rng, dims, jnp.float32) * scale * factor_of
    return jnp.minimum(jnp.maximum(result, -bound), bound).astype(held_as)


def setup_inputs(seed: int = 0) -> dict:
    arg_keys = jax.random.split(jax.random.key(seed), 7)
    tokens = normal_values(arg_keys[0], (TOKENS, D), 1.0, 6.0, ((0, 16), (1, 8)))
    cotangent = normal_values(arg_keys[1], (TOKENS, D), 1.0, 6.0, ((0, 16), (1, 8)))
    bleu_gains = draw_bleu_gains(jax.random.fold_in(arg_keys[6], 71), 0)
    gate_weight = normal_values(arg_keys[3], (D, FF), D ** -0.5, 0.0625, ((0, 8), (1, 16)))
    up_weight = normal_values(arg_keys[4], (D, FF), D ** -0.5, 0.0625, ((0, 8), (1, 16)))
    down_weight = normal_values(arg_keys[5], (FF, D), FF ** -0.5, 0.03125, ((0, 16), (1, 8)))
    return {"tokens": tokens, "cotangent": cotangent, "bleu_gains": bleu_gains, "gate_weight": gate_weight, "up_weight": up_weight, "down_weight": down_weight}


def swiglu_backward(back_sum, gate_sum, up_sum):
    sigmoid_gate = jax.nn.sigmoid(gate_sum)
    grad_gate = (back_sum * up_sum * sigmoid_gate * (1.0 + gate_sum * (1.0 - sigmoid_gate))).astype(jnp.bfloat16)
    grad_up = (back_sum * (gate_sum * sigmoid_gate)).astype(jnp.bfloat16)
    return grad_gate, grad_up


def reference(tokens, cotangent, bleu_gains, gate_weight, up_weight, down_weight):
    shifted = (bleu_gains + 1).astype(jnp.float32)
    risk_share = CANDS * shifted / jnp.sum(shifted, axis=1, keepdims=True)
    row_scale = jnp.repeat(risk_share.reshape(-1), LEN)
    grad_out = (row_scale[:, None] * cotangent).astype(jnp.bfloat16)
    gate_sum = jnp.dot(tokens, gate_weight, preferred_element_type=jnp.float32)
    up_sum = jnp.dot(tokens, up_weight, preferred_element_type=jnp.float32)
    hidden = (gate_sum * jax.nn.sigmoid(gate_sum) * up_sum).astype(jnp.bfloat16)
    layer_out = jnp.dot(hidden, down_weight, preferred_element_type=jnp.float32).astype(jnp.bfloat16)
    back_sum = jnp.dot(grad_out, down_weight.T, preferred_element_type=jnp.float32)
    grad_gate, grad_up = swiglu_backward(back_sum, gate_sum, up_sum)
    grad_down_weight = jnp.dot(hidden.T, grad_out, preferred_element_type=jnp.float32).astype(jnp.bfloat16)
    grad_gate_weight = jnp.dot(tokens.T, grad_gate, preferred_element_type=jnp.float32).astype(jnp.bfloat16)
    grad_up_weight = jnp.dot(tokens.T, grad_up, preferred_element_type=jnp.float32).astype(jnp.bfloat16)
    grad_tokens = (jnp.dot(grad_gate, gate_weight.T, preferred_element_type=jnp.float32)
                   + jnp.dot(grad_up, up_weight.T, preferred_element_type=jnp.float32)).astype(jnp.bfloat16)
    return layer_out, grad_tokens, grad_gate_weight, grad_up_weight, grad_down_weight
```

```python
import jax
import jax.numpy as jnp
from jax import lax
from jax.sharding import Mesh, PartitionSpec as P

CANDS = 8
BF16 = jnp.bfloat16
F32 = jnp.float32
FINE = ("zlo", "x", "y", "zhi", "core")
FSDP = ("zlo", "x")
HIDDEN = ("y", "zhi", "core")
COLS = (((1,), (1,)), ((), ()))
ROWS = (((0,), (0,)), ((), ()))


def swap(block, axis):
    return lax.ppermute(block, axis, [(0, 1), (1, 0)])


def shift(block, axis, step):
    n = lax.axis_size(axis)
    return lax.ppermute(block, axis, [(i, (i + step) % n) for i in range(n)])


def gather_near(block):
    pair = jnp.concatenate([block, swap(block, "zhi")], axis=0)
    ring = [pair] + [shift(pair, "y", k) for k in (1, 2, 3)]
    mine = jnp.concatenate(ring, axis=0)
    return mine, swap(mine, "core")


def scatter_near(keep, give):
    rows = keep.shape[0] // 8
    own = keep + swap(give.astype(BF16), "core").astype(F32)
    own = own.reshape(4, 2 * rows, -1)
    got = [shift(own[k].astype(BF16), "y", -k) for k in (1, 2, 3)]
    own = own[0] + (got[0].astype(F32) + got[1].astype(F32)) + got[2].astype(F32)
    return own[:rows] + swap(own[rows:].astype(BF16), "zhi").astype(F32)


def exchange_x(part):
    i = lax.axis_index("x")
    got = []
    for k in (1, 3, 2):
        block = lax.dynamic_index_in_dim(part, (i + k) % 4, 1, False).astype(BF16)
        got.append(shift(block, "x", k))
    own = lax.dynamic_index_in_dim(part, i, 1, False)
    return own + got[0].astype(F32) + got[1].astype(F32) + got[2].astype(F32)


def reduce_z_first(mine, other):
    half = mine + swap(other.astype(BF16), "zlo").astype(F32)
    return exchange_x(half.reshape(1, 4, -1, half.shape[1]))[0]


def reduce_x_first(mine, other):
    n = mine.shape[1]
    pair = exchange_x(jnp.stack([mine, other]).reshape(2, 4, -1, n))
    return pair[0] + swap(pair[1].astype(BF16), "zlo").astype(F32)


def spread_x(block):
    return lax.all_gather(block, "x", axis=0, tiled=True)


def swiglu_backward(back_sum, gate_sum, up_sum):
    sigmoid_gate = jax.nn.sigmoid(gate_sum)
    grad_gate = (back_sum * up_sum * sigmoid_gate * (1.0 + gate_sum * (1.0 - sigmoid_gate))).astype(BF16)
    grad_up = (back_sum * (gate_sum * sigmoid_gate)).astype(BF16)
    return (grad_gate, grad_up)


def swiglu_forward(gate_sum, up_sum):
    return (gate_sum * jax.nn.sigmoid(gate_sum) * up_sum).astype(BF16)


def dot(a, b, dims=(((1,), (0,)), ((), ()))):
    return lax.dot_general(a, b, dims, preferred_element_type=F32)


def on_device(tokens, cotangent, bleu_gains, gate_weight, up_weight, down_weight):
    seq_len = tokens.shape[0] // bleu_gains.size
    low = lax.axis_index("zlo") == 0

    def by_z(a, b):
        return jnp.where(low, a, b), jnp.where(low, b, a)

    tok = jnp.concatenate(by_z(*gather_near(tokens)), axis=0)
    shifted = (bleu_gains + 1).astype(F32)
    totals = jnp.sum(shifted, axis=1, keepdims=True)
    totals = totals + swap(totals, "zhi")
    totals = totals + swap(totals, "core")
    row_scale = jnp.repeat((CANDS * shifted / totals).reshape(-1), seq_len)
    grad_own = (row_scale[:, None] * cotangent).astype(BF16)
    grad = jnp.concatenate(by_z(*gather_near(grad_own)), axis=0)
    h = tok.shape[0] // 2

    gate_part = dot(tok, gate_weight)
    up_part = dot(tok, up_weight)
    back_part = dot(grad, down_weight, COLS)
    gate_sum = reduce_z_first(gate_part[:h], gate_part[h:])
    up_sum = reduce_x_first(up_part[:h], up_part[h:])
    back_sum = reduce_z_first(back_part[:h], back_part[h:])

    hidden = swiglu_forward(gate_sum, up_sum)
    hid_mine = spread_x(hidden)
    hid_other = swap(hid_mine, "zlo")
    grad_gate, grad_up = swiglu_backward(back_sum, gate_sum, up_sum)
    gg_mine = spread_x(grad_gate)
    gg_other = swap(gg_mine, "zlo")
    gu_mine = spread_x(grad_up)
    gu_other = spread_x(swap(grad_up, "zlo"))
    hid = jnp.concatenate([hid_mine, hid_other], axis=0)
    gg = jnp.concatenate([gg_mine, gg_other], axis=0)
    gu = jnp.concatenate([gu_mine, gu_other], axis=0)

    out_part = dot(hid, down_weight)
    layer_out = scatter_near(*by_z(out_part[:h], out_part[h:])).astype(BF16)
    grad_down_weight = dot(hid, grad, ROWS).astype(BF16)
    grad_up_weight = dot(tok, gu, ROWS).astype(BF16)
    grad_gate_weight = dot(tok, gg, ROWS).astype(BF16)
    tok_part = dot(gg, gate_weight, COLS) + dot(gu, up_weight, COLS)
    grad_tokens = scatter_near(*by_z(tok_part[:h], tok_part[h:])).astype(BF16)
    return (layer_out, grad_tokens, grad_gate_weight, grad_up_weight, grad_down_weight)


def solution(mesh):
    fine = Mesh(mesh.devices.reshape(2, 4, 4, 2, 2), FINE)
    rows = P(HIDDEN, FSDP)
    return jax.shard_map(
        on_device,
        mesh=fine,
        in_specs=(rows, rows, P("y", ("zhi", "core")), P(FSDP, HIDDEN), P(FSDP, HIDDEN), rows),
        out_specs=(rows, rows, P(FSDP, HIDDEN), P(FSDP, HIDDEN), rows),
        check_vma=False,
    )
```

```python
import jax
import jax.numpy as jnp
from jax import lax
from jax.experimental.layout import Layout, with_layout_constraint
from jax.sharding import Mesh, PartitionSpec as P

CANDS = 8
BF16 = jnp.bfloat16
F32 = jnp.float32
FINE = ("zlo", "x", "y", "zhi", "core")
FSDP = ("zlo", "x")
HIDDEN = ("y", "zhi", "core")
COLS = (((1,), (1,)), ((), ()))
ROWS = (((0,), (0,)), ((), ()))


def swap(block, axis):
    return lax.ppermute(block, axis, [(0, 1), (1, 0)])


def shift(block, axis, step):
    n = lax.axis_size(axis)
    return lax.ppermute(block, axis, [(i, (i + step) % n) for i in range(n)])


def gather_near(block):
    pair = jnp.concatenate([block, swap(block, "zhi")], axis=0)
    ring = [pair] + [shift(pair, "y", k) for k in (1, 2, 3)]
    mine = jnp.concatenate(ring, axis=0)
    return mine, swap(mine, "core")


def scatter_near(part):
    d = part.shape[1]
    low = lax.axis_index("zlo") == 0
    i = lax.axis_index("x")
    half = part.reshape(2, -1, d)
    give = jnp.where(low, half[1], half[0]).astype(BF16)
    own = jnp.where(low, half[0], half[1]) + swap(give, "core").astype(F32)
    own = own.reshape(4, -1, d)

    def block(k):
        return lax.dynamic_index_in_dim(own, (k - i) % 4, 0, False)

    got = [shift(block(k).astype(BF16), "y", -k) for k in (1, 2, 3)]
    mine = block(0) + (got[0].astype(F32) + got[1].astype(F32)) + got[2].astype(F32)
    rows = mine.shape[0] // 2
    return mine[:rows] + swap(mine[rows:].astype(BF16), "zhi").astype(F32)


def exchange_x(part):
    i = lax.axis_index("x")
    got = []
    for k in (1, 3, 2):
        block = lax.dynamic_index_in_dim(part, (i + k) % 4, 1, False).astype(BF16)
        got.append(shift(block, "x", k))
    own = lax.dynamic_index_in_dim(part, i, 1, False)
    return own + got[0].astype(F32) + got[1].astype(F32) + got[2].astype(F32)


def reduce_z_first(mine, other):
    half = mine + swap(other.astype(BF16), "zlo").astype(F32)
    return exchange_x(half.reshape(1, 4, -1, half.shape[1]))[0]


def reduce_x_first(mine, other):
    n = mine.shape[1]
    pair = exchange_x(jnp.stack([mine, other]).reshape(2, 4, -1, n))
    return pair[0] + swap(pair[1].astype(BF16), "zlo").astype(F32)


def gather_x_first(block):
    near = swap(block, "zlo")
    far = jnp.concatenate([shift(block, "x", -k) for k in (1, 2, 3)], axis=0)
    return jnp.concatenate([block, far, near, swap(far, "zlo")], axis=0)


def gather_z_first(block):
    pair = jnp.stack([block, swap(block, "zlo")])
    all_x = jnp.stack([pair] + [shift(pair, "x", -k) for k in (1, 2, 3)], axis=1)
    return all_x.reshape(-1, block.shape[1])


def by_relative_x(rows):
    d = rows.shape[1]
    blocks = rows.reshape(2, 4, -1, d)
    twice = jnp.concatenate([blocks, blocks], axis=1)
    return lax.dynamic_slice_in_dim(twice, lax.axis_index("x"), 4, 1).reshape(-1, d)


def row_major(a):
    return with_layout_constraint(a, Layout((0, 1)))


def swiglu_backward(back_sum, gate_sum, up_sum):
    sigmoid_gate = jax.nn.sigmoid(gate_sum)
    grad_gate = (back_sum * up_sum * sigmoid_gate * (1.0 + gate_sum * (1.0 - sigmoid_gate))).astype(BF16)
    grad_up = (back_sum * (gate_sum * sigmoid_gate)).astype(BF16)
    return (grad_gate, grad_up)


def swiglu_forward(gate_sum, up_sum):
    return (gate_sum * jax.nn.sigmoid(gate_sum) * up_sum).astype(BF16)


def dot(a, b, dims=(((1,), (0,)), ((), ()))):
    return lax.dot_general(a, b, dims, preferred_element_type=F32)


def on_device(tokens, cotangent, bleu_gains, gate_weight, up_weight, down_weight):
    seq_len = tokens.shape[0] // bleu_gains.size
    low = lax.axis_index("zlo") == 0

    def by_z(a, b):
        return jnp.where(low, a, b), jnp.where(low, b, a)

    tok = jnp.concatenate(by_z(*gather_near(tokens)), axis=0)
    shifted = (bleu_gains + 1).astype(F32)
    totals = jnp.sum(shifted, axis=1, keepdims=True)
    totals = totals + swap(totals, "zhi")
    totals = totals + swap(totals, "core")
    row_scale = jnp.repeat((CANDS * shifted / totals).reshape(-1), seq_len)
    grad_own = (row_scale[:, None] * cotangent).astype(BF16)
    grad = jnp.concatenate(by_z(*gather_near(grad_own)), axis=0)
    h = tok.shape[0] // 2

    gate_part = row_major(dot(tok, gate_weight))
    up_part = row_major(dot(tok, up_weight))
    back_part = row_major(dot(grad, down_weight, COLS))
    gate_sum = reduce_z_first(gate_part[:h], gate_part[h:])
    up_sum = reduce_x_first(up_part[:h], up_part[h:])
    back_sum = reduce_z_first(back_part[:h], back_part[h:])
    tok = by_relative_x(tok)
    grad = by_relative_x(grad)

    hid = gather_x_first(swiglu_forward(gate_sum, up_sum))
    layer_out = scatter_near(dot(hid, down_weight)).astype(BF16)
    grad_down_weight = dot(hid, grad, ROWS).astype(BF16)
    grad_gate, grad_up = swiglu_backward(back_sum, gate_sum, up_sum)
    gg = gather_z_first(grad_gate)
    gu = gather_x_first(grad_up)
    grad_gate_weight = dot(tok, gg, ROWS).astype(BF16)
    grad_up_weight = dot(tok, gu, ROWS).astype(BF16)
    tok_part = dot(gg, gate_weight, COLS) + dot(gu, up_weight, COLS)
    grad_tokens = scatter_near(tok_part).astype(BF16)
    return (layer_out, grad_tokens, grad_gate_weight, grad_up_weight, grad_down_weight)


def solution(mesh):
    fine = Mesh(mesh.devices.reshape(2, 4, 4, 2, 2), FINE)
    rows = P(HIDDEN, FSDP)
    return jax.shard_map(
        on_device,
        mesh=fine,
        in_specs=(rows, rows, P("y", ("zhi", "core")), P(FSDP, HIDDEN), P(FSDP, HIDDEN), rows),
        out_specs=(rows, rows, P(FSDP, HIDDEN), P(FSDP, HIDDEN), rows),
        check_vma=False,
    )
```

```python
import jax
import jax.numpy as jnp
from jax import lax
from jax.experimental.layout import Layout, with_layout_constraint
from jax.sharding import Mesh, PartitionSpec as P

CANDS = 8
BF16 = jnp.bfloat16
F32 = jnp.float32
FINE = ("zlo", "x", "y", "zhi", "core")
FSDP = ("zlo", "x")
HIDDEN = ("y", "zhi", "core")
COLS = (((1,), (1,)), ((), ()))
ROWS = (((0,), (0,)), ((), ()))


def after(block, *others):
    return lax.optimization_barrier((block,) + others)[0]


def swap(block, axis):
    return lax.ppermute(block, axis, [(0, 1), (1, 0)])


def shift(block, axis, step):
    n = lax.axis_size(axis)
    return lax.ppermute(block, axis, [(i, (i + step) % n) for i in range(n)])


def ring_near(pair):
    return [pair] + [shift(pair, "y", k) for k in (1, 2, 3)]


def join_near(ring, *others):
    mine = after(jnp.concatenate(ring, axis=0), *others)
    return mine, swap(mine, "core")


def scale_rows(mine, other, rows, seq_len):
    d = mine.shape[1]
    both = jnp.stack([mine, other]).reshape(2, 4, -1, d)
    gains = both[:, :, 2 * rows :: 16, : 2 * rows // seq_len].astype(F32).reshape(2, 4, 2, 2, -1)
    shifted = gains[:, :, :, 0] * 128.0 + gains[:, :, :, 1]
    totals = jnp.sum(shifted, axis=(0, 2, 3), keepdims=True)
    row_scale = jnp.repeat((CANDS * shifted / totals).reshape(2, 4, -1), seq_len, axis=2)
    grad = (row_scale[..., None] * both[:, :, : 2 * rows]).astype(BF16).reshape(2, -1, d)
    return grad[0], grad[1]


def scatter_ring(low_half, high_half, i):
    d = low_half.shape[1]
    own = low_half + swap(high_half.astype(BF16), "core").astype(F32)
    own = own.reshape(4, -1, d)

    def block(k):
        return lax.dynamic_index_in_dim(own, (k - i) % 4, 0, False)

    got = [shift(block(k).astype(BF16), "y", -k) for k in (1, 2, 3)]
    return block(0) + (got[0].astype(F32) + got[1].astype(F32)) + got[2].astype(F32)


def scatter_pair(mine):
    rows = mine.shape[0] // 2
    return mine[:rows] + swap(mine[rows:].astype(BF16), "zhi").astype(F32)


def send_x(part):
    i = lax.axis_index("x")
    got = []
    for k in (1, 3, 2):
        block = lax.dynamic_index_in_dim(part, (i + k) % 4, 1, False).astype(BF16)
        got.append(shift(block, "x", k))
    return lax.dynamic_index_in_dim(part, i, 1, False), got


def add_x(own, got):
    return own + got[0].astype(F32) + got[1].astype(F32) + got[2].astype(F32)


def gather_z_first(block):
    pair = jnp.stack([block, swap(block, "zlo")])
    all_x = jnp.stack([pair] + [shift(pair, "x", -k) for k in (1, 2, 3)], axis=1)
    return all_x.reshape(-1, block.shape[1])


def far_x(block):
    return jnp.concatenate([shift(block, "x", -k) for k in (1, 2, 3)], axis=0)


def by_relative_x(rows):
    d = rows.shape[1]
    blocks = rows.reshape(2, 4, -1, d)
    twice = jnp.concatenate([blocks, blocks], axis=1)
    return lax.dynamic_slice_in_dim(twice, lax.axis_index("x"), 4, 1).reshape(-1, d)


def row_major(a):
    return with_layout_constraint(a, Layout((0, 1)))


def swiglu_backward(back_sum, gate_sum, up_sum):
    sigmoid_gate = jax.nn.sigmoid(gate_sum)
    grad_gate = (back_sum * up_sum * sigmoid_gate * (1.0 + gate_sum * (1.0 - sigmoid_gate))).astype(BF16)
    grad_up = (back_sum * (gate_sum * sigmoid_gate)).astype(BF16)
    return (grad_gate, grad_up)


def swiglu_forward(gate_sum, up_sum):
    return (gate_sum * jax.nn.sigmoid(gate_sum) * up_sum).astype(BF16)


def dot(a, b, dims=(((1,), (0,)), ((), ()))):
    return lax.dot_general(a, b, dims, preferred_element_type=F32)


def on_device(tokens, cotangent, bleu_gains, gate_weight, up_weight, down_weight):
    seq_len = tokens.shape[0] // bleu_gains.size
    low = lax.axis_index("zlo") == 0

    def by_z(a, b):
        return jnp.where(low, a, b), jnp.where(low, b, a)

    rows = tokens.shape[0]
    shifted = bleu_gains.reshape(1, -1) + 1
    gains = jnp.concatenate([shifted >> 7, shifted & 127], axis=1).astype(BF16)
    gains = jnp.pad(gains, ((0, 15), (0, tokens.shape[1] - gains.shape[1])))
    own = jnp.concatenate([tokens, cotangent, gains], axis=0)
    near = swap(own, "zhi")
    tok_pair = jnp.concatenate([tokens, near[:rows]], axis=0)
    grad_pair = jnp.concatenate([cotangent, near[rows : 2 * rows], gains, near[2 * rows :]], axis=0)
    tok_ring = ring_near(tok_pair)
    grad_ring = ring_near(grad_pair)
    tok = jnp.concatenate(by_z(*join_near(tok_ring)), axis=0)
    h = tok.shape[0] // 2
    n = gate_weight.shape[1]

    gate_part = row_major(dot(tok, gate_weight))
    gate_give = gate_part[h:].astype(BF16)
    gate_near = swap(gate_give, "zlo")
    up_part = row_major(dot(after(tok, gate_give), up_weight))
    up_own, up_got = send_x(up_part.reshape(2, 4, -1, n))

    grad_ring = lax.optimization_barrier((*grad_ring, gate_give))[:4]
    grad_halves = scale_rows(*join_near(grad_ring), rows, seq_len)
    grad = jnp.concatenate(by_z(*grad_halves), axis=0)
    back_part = row_major(dot(grad, down_weight, COLS))
    back_give = back_part[h:].astype(BF16)
    back_first, back_last = swap(back_give[: h // 4], "zlo"), swap(back_give[h // 4 :], "zlo")
    gate_half = gate_part[:h] + gate_near.astype(F32)
    gate_own, gate_got = send_x(gate_half.reshape(1, 4, -1, n))
    *up_got, _ = lax.optimization_barrier((*up_got, back_first))
    up_pair = add_x(up_own, up_got)
    up_near = swap(up_pair[1].astype(BF16), "zlo")

    back_near = jnp.concatenate([back_first, after(back_last, *gate_got)], axis=0)
    back_half = back_part[:h] + back_near.astype(F32)
    back_own, back_got = send_x(back_half.reshape(1, 4, -1, n))
    gate_sum = add_x(gate_own, gate_got)[0]
    up_sum = up_pair[0] + up_near.astype(F32)
    hidden = swiglu_forward(gate_sum, up_sum)
    hid_near = swap(hidden, "zlo")
    hid_far = far_x(hidden)
    hid_both = swap(hid_far, "zlo")
    *back_got, _ = lax.optimization_barrier((*back_got, hidden))
    back_sum = add_x(back_own, back_got)[0]
    tok = by_relative_x(tok)
    grad = by_relative_x(grad)
    grad_gate, grad_up = swiglu_backward(back_sum, gate_sum, up_sum)
    gg = gather_z_first(grad_gate)
    gu_far = far_x(grad_up)
    gu_near = swap(grad_up, "zlo")
    gu_both = swap(gu_far, "zlo")

    hid = jnp.concatenate([hidden, hid_far, hid_near, hid_both], axis=0)
    out_part = dot(hid, down_weight)
    i = lax.axis_index("x")
    out_ring = scatter_ring(*by_z(out_part[:h], out_part[h:]), i)
    layer_out = scatter_pair(out_ring).astype(BF16)
    grad_down_weight = dot(hid, grad, ROWS).astype(BF16)
    gg = after(gg, out_ring, grad_down_weight)
    tok_part = dot(gg, gate_weight, COLS)
    gu_both = after(gu_both, tok_part)
    gu = jnp.concatenate([grad_up, gu_far, gu_near, gu_both], axis=0)
    tok_part = tok_part + dot(gu, up_weight, COLS)
    tok = after(tok, tok_part)
    grad_gate_weight = dot(tok, gg, ROWS).astype(BF16)
    grad_up_weight = dot(tok, gu, ROWS).astype(BF16)
    grad_tokens = scatter_pair(scatter_ring(*by_z(tok_part[:h], tok_part[h:]), i)).astype(BF16)
    return (layer_out, grad_tokens, grad_gate_weight, grad_up_weight, grad_down_weight)


def solution(mesh):
    fine = Mesh(mesh.devices.reshape(2, 4, 4, 2, 2), FINE)
    rows = P(HIDDEN, FSDP)
    return jax.shard_map(
        on_device,
        mesh=fine,
        in_specs=(rows, rows, P("y", ("zhi", "core")), P(FSDP, HIDDEN), P(FSDP, HIDDEN), rows),
        out_specs=(rows, rows, P(FSDP, HIDDEN), P(FSDP, HIDDEN), rows),
        check_vma=False,
    )
```

```python
import jax
import jax.numpy as jnp
from jax import lax
from jax.experimental.layout import Layout, with_layout_constraint
from jax.sharding import Mesh, PartitionSpec as P

CANDS = 8
BF16 = jnp.bfloat16
F32 = jnp.float32
FINE = ("zlo", "x", "y", "zhi", "core")
FSDP = ("zlo", "x")
HIDDEN = ("y", "zhi", "core")
COLS = (((1,), (1,)), ((), ()))
ROWS = (((0,), (0,)), ((), ()))


def after(block, *others):
    return lax.optimization_barrier((block,) + others)[0]


def swap(block, axis):
    return lax.ppermute(block, axis, [(0, 1), (1, 0)])


def shift(block, axis, step):
    n = lax.axis_size(axis)
    return lax.ppermute(block, axis, [(i, (i + step) % n) for i in range(n)])


def ring_near(pair):
    return [pair] + [shift(pair, "y", k) for k in (1, 2, 3)]


def join_near(ring, *others):
    mine = after(jnp.concatenate(ring, axis=0), *others)
    return mine, swap(mine, "core")


def scale_rows(mine, other, rows, seq_len):
    d = mine.shape[1]
    both = jnp.stack([mine, other]).reshape(2, 4, -1, d)
    gains = both[:, :, 2 * rows :: 16, : 2 * rows // seq_len].astype(F32).reshape(2, 4, 2, 2, -1)
    shifted = gains[:, :, :, 0] * 128.0 + gains[:, :, :, 1]
    totals = jnp.sum(shifted, axis=(0, 2, 3), keepdims=True)
    row_scale = jnp.repeat((CANDS * shifted / totals).reshape(2, 4, -1), seq_len, axis=2)
    grad = (row_scale[..., None] * both[:, :, : 2 * rows]).astype(BF16).reshape(2, -1, d)
    return grad[0], grad[1]


def scatter_ring(low_half, high_half, i):
    d = low_half.shape[1]
    own = low_half + swap(high_half.astype(BF16), "core").astype(F32)
    own = own.reshape(4, -1, d)

    def block(k):
        return lax.dynamic_index_in_dim(own, (k - i) % 4, 0, False)

    got = [shift(block(k).astype(BF16), "y", -k) for k in (1, 2, 3)]
    return block(0) + (got[0].astype(F32) + got[1].astype(F32)) + got[2].astype(F32)


def scatter_pair(mine):
    rows = mine.shape[0] // 2
    return mine[:rows] + swap(mine[rows:].astype(BF16), "zhi").astype(F32)


def send_x(part):
    i = lax.axis_index("x")
    got = []
    for k in (1, 3, 2):
        block = lax.dynamic_index_in_dim(part, (i + k) % 4, 1, False).astype(BF16)
        got.append(shift(block, "x", k))
    return lax.dynamic_index_in_dim(part, i, 1, False), got


def add_x(own, got):
    return own + got[0].astype(F32) + got[1].astype(F32) + got[2].astype(F32)


def gather_z_first(block):
    pair = jnp.stack([block, swap(block, "zlo")])
    all_x = jnp.stack([pair] + [shift(pair, "x", -k) for k in (1, 2, 3)], axis=1)
    return all_x.reshape(-1, block.shape[1])


def far_x(block):
    return jnp.concatenate([shift(block, "x", -k) for k in (1, 2, 3)], axis=0)


def by_relative_x(rows):
    d = rows.shape[1]
    blocks = rows.reshape(2, 4, -1, d)
    twice = jnp.concatenate([blocks, blocks], axis=1)
    return lax.dynamic_slice_in_dim(twice, lax.axis_index("x"), 4, 1).reshape(-1, d)


def row_major(a):
    return with_layout_constraint(a, Layout((0, 1)))


def swiglu_backward(back_sum, gate_sum, up_sum):
    sigmoid_gate = jax.nn.sigmoid(gate_sum)
    grad_gate = (back_sum * up_sum * sigmoid_gate * (1.0 + gate_sum * (1.0 - sigmoid_gate))).astype(BF16)
    grad_up = (back_sum * (gate_sum * sigmoid_gate)).astype(BF16)
    return (grad_gate, grad_up)


def swiglu_forward(gate_sum, up_sum):
    return (gate_sum * jax.nn.sigmoid(gate_sum) * up_sum).astype(BF16)


def dot(a, b, dims=(((1,), (0,)), ((), ()))):
    return lax.dot_general(a, b, dims, preferred_element_type=F32)


def on_device(tokens, cotangent, bleu_gains, gate_weight, up_weight, down_weight):
    seq_len = tokens.shape[0] // bleu_gains.size
    low = lax.axis_index("zlo") == 0

    def by_z(a, b):
        return jnp.where(low, a, b), jnp.where(low, b, a)

    rows = tokens.shape[0]
    shifted = bleu_gains.reshape(1, -1) + 1
    gains = jnp.concatenate([shifted >> 7, shifted & 127], axis=1).astype(BF16)
    gains = jnp.pad(gains, ((0, 15), (0, tokens.shape[1] - gains.shape[1])))
    own = jnp.concatenate([tokens, cotangent, gains], axis=0)
    near = swap(own, "zhi")
    tok_pair = jnp.concatenate([tokens, near[:rows]], axis=0)
    grad_pair = jnp.concatenate([cotangent, near[rows : 2 * rows], gains, near[2 * rows :]], axis=0)
    tok_ring = ring_near(tok_pair)
    grad_ring = ring_near(grad_pair)
    tok = jnp.concatenate(by_z(*join_near(tok_ring)), axis=0)
    h = tok.shape[0] // 2
    n = gate_weight.shape[1]

    gate_part = row_major(dot(tok, gate_weight))
    gate_give = gate_part[h:].astype(BF16)
    gate_near = swap(gate_give, "zlo")
    up_part = row_major(dot(after(tok, gate_give), up_weight))
    up_own, up_got = send_x(up_part.reshape(2, 4, -1, n))

    grad_ring = lax.optimization_barrier((*grad_ring, gate_give))[:4]
    grad_halves = scale_rows(*join_near(grad_ring), rows, seq_len)
    grad = jnp.concatenate(by_z(*grad_halves), axis=0)
    back_part = row_major(dot(grad, down_weight, COLS))
    back_give = back_part[h:].astype(BF16)
    back_first, back_last = swap(back_give[: h // 4], "zlo"), swap(back_give[h // 4 :], "zlo")
    gate_half = gate_part[:h] + gate_near.astype(F32)
    gate_own, gate_got = send_x(gate_half.reshape(1, 4, -1, n))
    *up_got, _ = lax.optimization_barrier((*up_got, back_first))
    up_pair = add_x(up_own, up_got)
    up_near = swap(up_pair[1].astype(BF16), "zlo")

    back_near = jnp.concatenate([back_first, after(back_last, *gate_got)], axis=0)
    back_half = back_part[:h] + back_near.astype(F32)
    back_own, back_got = send_x(back_half.reshape(1, 4, -1, n))
    gate_sum = add_x(gate_own, gate_got)[0]
    up_sum = up_pair[0] + up_near.astype(F32)
    hidden = swiglu_forward(gate_sum, up_sum)
    hid_near = swap(hidden, "zlo")
    hid_far = far_x(hidden)
    hid_both = swap(hid_far, "zlo")
    *back_got, _ = lax.optimization_barrier((*back_got, hidden))
    back_sum = add_x(back_own, back_got)[0]
    tok = by_relative_x(tok)
    grad = by_relative_x(grad)
    grad_gate, grad_up = swiglu_backward(back_sum, gate_sum, up_sum)
    gg = gather_z_first(grad_gate)
    gu_far = far_x(grad_up)
    gu_near = swap(grad_up, "zlo")
    gu_both = swap(gu_far, "zlo")

    hid = jnp.concatenate([hidden, hid_far, hid_near, hid_both], axis=0)
    out_part = dot(hid, down_weight)
    i = lax.axis_index("x")
    out_ring = scatter_ring(*by_z(out_part[:h], out_part[h:]), i)
    grad_down_weight = dot(hid, grad, ROWS).astype(BF16)
    gg = after(gg, out_ring, grad_down_weight)
    tok_part = dot(gg, gate_weight, COLS)
    gu_both = after(gu_both, tok_part)
    gu = jnp.concatenate([grad_up, gu_far, gu_near, gu_both], axis=0)
    tok_part = tok_part + dot(gu, up_weight, COLS)
    tok = after(tok, tok_part)
    grad_gate_weight = dot(tok, gg, ROWS).astype(BF16)
    grad_up_weight = dot(tok, gu, ROWS).astype(BF16)
    tok_ring = scatter_ring(*by_z(tok_part[:h], tok_part[h:]), i)
    both = scatter_pair(jnp.concatenate([out_ring, tok_ring], axis=1)).astype(BF16)
    layer_out, grad_tokens = jnp.split(both, 2, axis=1)
    return (layer_out, grad_tokens, grad_gate_weight, grad_up_weight, grad_down_weight)


def solution(mesh):
    fine = Mesh(mesh.devices.reshape(2, 4, 4, 2, 2), FINE)
    rows = P(HIDDEN, FSDP)
    return jax.shard_map(
        on_device,
        mesh=fine,
        in_specs=(rows, rows, P("y", ("zhi", "core")), P(FSDP, HIDDEN), P(FSDP, HIDDEN), rows),
        out_specs=(rows, rows, P(FSDP, HIDDEN), P(FSDP, HIDDEN), rows),
        check_vma=False,
    )
```

```python
import jax
import jax.numpy as jnp
from jax import lax
from jax.experimental.layout import Layout, with_layout_constraint
from jax.sharding import Mesh, PartitionSpec as P

CANDS = 8
BF16 = jnp.bfloat16
F32 = jnp.float32
FINE = ("zlo", "x", "y", "zhi", "core")
FSDP = ("zlo", "x")
HIDDEN = ("y", "zhi", "core")
COLS = (((1,), (1,)), ((), ()))
ROWS = (((0,), (0,)), ((), ()))


def after(block, *others):
    return lax.optimization_barrier((block,) + others)[0]


def swap(block, axis):
    return lax.ppermute(block, axis, [(0, 1), (1, 0)])


def shift(block, axis, step):
    n = lax.axis_size(axis)
    return lax.ppermute(block, axis, [(i, (i + step) % n) for i in range(n)])


def ring_near(pair):
    return [pair] + [shift(pair, "y", k) for k in (1, 2, 3)]


def join_near(ring, *others):
    mine = after(jnp.concatenate(ring, axis=0), *others)
    return mine, swap(mine, "core")


def scale_rows(mine, other, rows, seq_len):
    d = mine.shape[1]
    both = jnp.stack([mine, other]).reshape(2, 4, -1, d)
    gains = both[:, :, 2 * rows :: 16, : 2 * rows // seq_len].astype(F32).reshape(2, 4, 2, 2, -1)
    shifted = gains[:, :, :, 0] * 128.0 + gains[:, :, :, 1]
    totals = jnp.sum(shifted, axis=(0, 2, 3), keepdims=True)
    row_scale = jnp.repeat((CANDS * shifted / totals).reshape(2, 4, -1), seq_len, axis=2)
    grad = (row_scale[..., None] * both[:, :, : 2 * rows]).astype(BF16).reshape(2, -1, d)
    return grad[0], grad[1]


def scatter_ring(low_half, high_half, i):
    d = low_half.shape[1]
    own = low_half + swap(high_half.astype(BF16), "core").astype(F32)
    own = own.reshape(4, -1, d)

    def block(k):
        return lax.dynamic_index_in_dim(own, (k - i) % 4, 0, False)

    got = [shift(block(k).astype(BF16), "y", -k) for k in (1, 2, 3)]
    return block(0) + (got[0].astype(F32) + got[1].astype(F32)) + got[2].astype(F32)


def scatter_pair(mine):
    rows = mine.shape[0] // 2
    return mine[:rows] + swap(mine[rows:].astype(BF16), "zhi").astype(F32)


def send_x(part):
    i = lax.axis_index("x")
    got = []
    for k in (1, 3, 2):
        block = lax.dynamic_index_in_dim(part, (i + k) % 4, 1, False).astype(BF16)
        got.append(shift(block, "x", k))
    return lax.dynamic_index_in_dim(part, i, 1, False), got


def add_x(own, got):
    return own + got[0].astype(F32) + got[1].astype(F32) + got[2].astype(F32)


def gather_z_first(block):
    pair = jnp.stack([block, swap(block, "zlo")])
    all_x = jnp.stack([pair] + [shift(pair, "x", -k) for k in (1, 2, 3)], axis=1)
    return all_x.reshape(-1, block.shape[1])


def far_x(block):
    return jnp.concatenate([shift(block, "x", -k) for k in (1, 2, 3)], axis=0)


def by_relative_x(rows):
    d = rows.shape[1]
    blocks = rows.reshape(2, 4, -1, d)
    twice = jnp.concatenate([blocks, blocks], axis=1)
    return lax.dynamic_slice_in_dim(twice, lax.axis_index("x"), 4, 1).reshape(-1, d)


def row_major(a):
    return with_layout_constraint(a, Layout((0, 1)))


def swiglu_backward(back_sum, gate_sum, up_sum):
    sigmoid_gate = jax.nn.sigmoid(gate_sum)
    grad_gate = (back_sum * up_sum * sigmoid_gate * (1.0 + gate_sum * (1.0 - sigmoid_gate))).astype(BF16)
    grad_up = (back_sum * (gate_sum * sigmoid_gate)).astype(BF16)
    return (grad_gate, grad_up)


def swiglu_forward(gate_sum, up_sum):
    return (gate_sum * jax.nn.sigmoid(gate_sum) * up_sum).astype(BF16)


def dot(a, b, dims=(((1,), (0,)), ((), ()))):
    return lax.dot_general(a, b, dims, preferred_element_type=F32)


def on_device(tokens, cotangent, bleu_gains, gate_weight, up_weight, down_weight):
    seq_len = tokens.shape[0] // bleu_gains.size
    low = lax.axis_index("zlo") == 0

    def by_z(a, b):
        return jnp.where(low, a, b), jnp.where(low, b, a)

    rows = tokens.shape[0]
    shifted = bleu_gains.reshape(1, -1) + 1
    gains = jnp.concatenate([shifted >> 7, shifted & 127], axis=1).astype(BF16)
    gains = jnp.pad(gains, ((0, 15), (0, tokens.shape[1] - gains.shape[1])))
    own = jnp.concatenate([tokens, cotangent, gains], axis=0)
    near = swap(own, "zhi")
    tok_pair = jnp.concatenate([tokens, near[:rows]], axis=0)
    grad_pair = jnp.concatenate([cotangent, near[rows : 2 * rows], gains, near[2 * rows :]], axis=0)
    tok_ring = ring_near(tok_pair)
    grad_ring = ring_near(grad_pair)
    tok = jnp.concatenate(by_z(*join_near(tok_ring)), axis=0)
    h = tok.shape[0] // 2
    n = gate_weight.shape[1]

    gate_part = row_major(dot(tok, gate_weight))
    gate_give = gate_part[h:].astype(BF16)
    gate_near = swap(gate_give, "zlo")
    up_part = row_major(dot(after(tok, gate_give), up_weight))
    up_own, up_got = send_x(up_part.reshape(2, 4, -1, n))

    grad_ring = lax.optimization_barrier((*grad_ring, gate_give))[:4]
    grad_halves = scale_rows(*join_near(grad_ring), rows, seq_len)
    grad = jnp.concatenate(by_z(*grad_halves), axis=0)
    back_part = row_major(dot(grad, down_weight, COLS))
    back_give = back_part[h:].astype(BF16)
    back_first, back_last = swap(back_give[: h // 4], "zlo"), swap(back_give[h // 4 :], "zlo")
    gate_half = gate_part[:h] + gate_near.astype(F32)
    gate_own, gate_got = send_x(gate_half.reshape(1, 4, -1, n))
    *up_got, _ = lax.optimization_barrier((*up_got, back_first))
    up_pair = add_x(up_own, up_got)
    up_near = swap(up_pair[1].astype(BF16), "zlo")

    back_near = jnp.concatenate([back_first, after(back_last, *gate_got)], axis=0)
    back_half = back_part[:h] + back_near.astype(F32)
    back_own, back_got = send_x(back_half.reshape(1, 4, -1, n))
    gate_sum = add_x(gate_own, gate_got)[0]
    up_sum = up_pair[0] + up_near.astype(F32)
    hidden = swiglu_forward(gate_sum, up_sum)
    hid_near = swap(hidden, "zlo")
    hid_far = far_x(after(hidden, back_own))
    hid_both = swap(hid_far, "zlo")
    *back_got, _ = lax.optimization_barrier((*back_got, hidden))
    back_sum = add_x(back_own, back_got)[0]
    tok = by_relative_x(tok)
    grad = by_relative_x(grad)
    grad_gate, grad_up = swiglu_backward(back_sum, gate_sum, up_sum)
    gg = gather_z_first(grad_gate)
    gu_far = far_x(grad_up)
    gu_near = swap(grad_up, "zlo")
    gu_both = swap(gu_far, "zlo")

    hid = jnp.concatenate([hidden, hid_far, hid_near, hid_both], axis=0)
    out_part = dot(hid, down_weight)
    i = lax.axis_index("x")
    out_ring = scatter_ring(*by_z(out_part[:h], out_part[h:]), i)
    grad_down_weight = dot(hid, grad, ROWS).astype(BF16)
    gg = after(gg, out_ring, grad_down_weight)
    tok_part = dot(gg, gate_weight, COLS)
    gu_both = after(gu_both, tok_part)
    gu = jnp.concatenate([grad_up, gu_far, gu_near, gu_both], axis=0)
    tok_part = tok_part + dot(gu, up_weight, COLS)
    tok = after(tok, tok_part)
    grad_gate_weight = dot(tok, gg, ROWS).astype(BF16)
    grad_up_weight = dot(tok, gu, ROWS).astype(BF16)
    tok_ring = scatter_ring(*by_z(tok_part[:h], tok_part[h:]), i)
    both = scatter_pair(jnp.concatenate([out_ring, tok_ring], axis=1)).astype(BF16)
    layer_out, grad_tokens = jnp.split(both, 2, axis=1)
    return (layer_out, grad_tokens, grad_gate_weight, grad_up_weight, grad_down_weight)


def solution(mesh):
    fine = Mesh(mesh.devices.reshape(2, 4, 4, 2, 2), FINE)
    rows = P(HIDDEN, FSDP)
    return jax.shard_map(
        on_device,
        mesh=fine,
        in_specs=(rows, rows, P("y", ("zhi", "core")), P(FSDP, HIDDEN), P(FSDP, HIDDEN), rows),
        out_specs=(rows, rows, P(FSDP, HIDDEN), P(FSDP, HIDDEN), rows),
        check_vma=False,
    )
```
